32 devices in a mesh: tile: 16 (over z, y, x), day: 2 (over core).
Axes of the slice: x: 2, y: 2, z: 4, core: 2. Of those that a mesh axis runs over, the one named last changes fastest.
Arguments:
- spectra: bfloat16 [2, 4096, 2, 4, 512], P('day', 'tile'), may hold values from -500 to 500
- band_low: int32 [32], P('tile'), may hold values from 0 to 127
- band_high: int32 [32], P('tile'), may hold values from 384 to 512
- pair_list: int32 [64, 2], P('tile'), may hold values from -1 to 31, as said below
Outputs:
- correlations: float32 [2, 64, 128, 128], P('day', 'tile')
The draws below stay inside these ranges and needn't reach their ends.
Inputs may be any that keep to these rules, and one draw needn't show every extreme that they name: `pair_list`: row p is either a pair (a, b) with 2 * (p // 4) <= a < 2 * (p // 4) + 2 and 0 <= b - a <= 6, or (-1, -1). In each aligned run of 4 rows the pairs come first, there is at least one, and in every draw some run holds 4 pairs.
All inputs are finite; a program needn't handle non-finite values.
Results may differ from the reference program's by a relative error of at most 0.0027.
Values may be sent and summed in bfloat16 or wider, within the bound.
A program may use at most 128 MiB of HBM per device.

```python
import math
import jax
import jax.numpy as jnp
from jax import lax

BLOCK = 128
BLK_DEV = 2
NF = 512
SEGLEN = 15000
FIRST = 90
HALF_WIN = 64
SEGS = 4
MAXOFF = 6
PAIR_DEV = 4
LSTEP = 25
NB = 32
CHANNELS = 4096
PAIRS = 64
DAYS = 2
LAGS = 2


def draw_spectra(key, part):
    first_key, second_key, third_key = jax.random.split(key, 3)
    full_shape = (DAYS, CHANNELS, 2, SEGS, NF)
    base_values = jnp.clip(jax.random.normal(first_key, full_shape, jnp.float32), -5.0, 5.0)
    log_range = jnp.log(10.0)
    row_scale = jnp.exp(jax.random.uniform(second_key, (DAYS, CHANNELS, 1, SEGS, 1), jnp.float32) * log_range)
    bin_scale = jnp.exp(jax.random.uniform(third_key, (DAYS, 1, 1, 1, NF), jnp.float32) * log_range)
    return (base_values * row_scale * bin_scale).astype(jnp.bfloat16)


def draw_pair_list(key, part):
    first_key, second_key, third_key, fourth_key = jax.random.split(key, 4)
    tile_count = NB // BLK_DEV
    row_index = jnp.arange(PAIRS, dtype=jnp.int32)
    tile_of_row = row_index // PAIR_DEV
    slot_of_row = row_index % PAIR_DEV
    live_counts = jax.random.randint(first_key, (tile_count,), 1, PAIR_DEV + 1)
    full_tile = jax.random.randint(second_key, (), 0, tile_count)
    live_counts = jnp.where(jnp.arange(tile_count, dtype=jnp.int32) == full_tile, PAIR_DEV, live_counts)
    first_block = BLK_DEV * tile_of_row + jax.random.randint(third_key, (PAIRS,), 0, BLK_DEV)
    second_block = jnp.minimum(first_block + jax.random.randint(fourth_key, (PAIRS,), 0, MAXOFF + 1), NB - 1)
    valid = slot_of_row < live_counts[tile_of_row]
    return jnp.stack([jnp.where(valid, first_block, -1), jnp.where(valid, second_block, -1)], axis=1).astype(jnp.int32)


def touch_ends(values, own_key, smallest, largest):
    spot = [jax.random.randint(jax.random.fold_in(own_key, axis), (), 0, length) for axis, length in enumerate(values.shape)]
    longest = values.shape.index(max(values.shape))
    beside = spot[:longest] + [(spot[longest] + 1) % values.shape[longest]] + spot[longest + 1:]
    return values.at[tuple(spot)].set(smallest).at[tuple(beside)].set(largest)


def setup_inputs(seed: int = 0) -> dict:
    arg_keys = jax.random.split(jax.random.key(seed), 5)
    return {
        "spectra": draw_spectra(jax.random.fold_in(arg_keys[4], 71), 0),
        "band_low": touch_ends(jax.random.randint(arg_keys[1], (NB,), 0, NF // 4), jax.random.fold_in(arg_keys[1], 1), 0, (NF // 4) - 1).astype(jnp.int32),
        "band_high": touch_ends(jax.random.randint(arg_keys[2], (NB,), 3 * NF // 4, NF + 1), jax.random.fold_in(arg_keys[2], 1), 3 * NF // 4, NF).astype(jnp.int32),
        "pair_list": draw_pair_list(jax.random.fold_in(arg_keys[4], 71), 0),
    }


def spread_mean(magnitude, bin_count):
    bin_index = jnp.arange(bin_count, dtype=jnp.int32)
    spread_matrix = (jnp.abs(bin_index[:, None] - bin_index[None, :]) <= HALF_WIN).astype(jnp.float32)
    bin_counts = lax.optimization_barrier(jnp.sum(spread_matrix, axis=0))
    flattened = magnitude.reshape(-1, bin_count)
    window_sums = jnp.dot(flattened, spread_matrix, precision=lax.Precision.HIGHEST)
    return (window_sums / bin_counts).reshape(magnitude.shape) + 1e-05

def whiten(raw):
    values = raw.astype(jnp.float32)
    magnitude = jnp.sqrt(values[:, 0] * values[:, 0] + values[:, 1] * values[:, 1])
    amplitude = spread_mean(magnitude, raw.shape[-1])
    return (values / amplitude[:, None]).astype(jnp.bfloat16)

def phase_tables(first_lag, lag_total, all_lags, bin_count):
    lag_index = first_lag + jnp.arange(lag_total, dtype=jnp.int32)
    lag_samples = (lag_index - all_lags // 2) * LSTEP
    bin_number = FIRST + jnp.arange(bin_count, dtype=jnp.int32)
    phase_turns = lag_samples[:, None] * bin_number[None, :] % SEGLEN
    phase_angle = phase_turns.astype(jnp.float32) * (2.0 * math.pi / SEGLEN)
    return (jnp.cos(phase_angle), jnp.sin(phase_angle))

def reference(spectra, band_low, band_high, pair_list):
    whitened = lax.map(whiten, spectra)
    blocks = whitened.reshape(DAYS, NB, BLOCK, 2, SEGS, NF)
    bin_index = jnp.arange(NF, dtype=jnp.int32)
    keep_mask = ((bin_index[None, :] >= band_low[:, None]) & (bin_index[None, :] < band_high[:, None])).astype(jnp.float32)
    cosine, sine_part = phase_tables(0, LAGS, LAGS, NF)
    norm_factor = 1.0 / math.sqrt(SEGS * NF * DAYS)

    def correlate(pair_row):
        first_block = jnp.maximum(pair_row[0], 0)
        second_block = jnp.maximum(pair_row[1], 0)
        left_block = blocks[:, first_block]
        partner = blocks[:, second_block].astype(jnp.float32)
        joint_keep = keep_mask[first_block] * keep_mask[second_block]
        cos_joint = (cosine * joint_keep)[None, :, None, None, :]
        sin_joint = (sine_part * joint_keep)[None, :, None, None, :]
        real_part = partner[:, None, :, 0]
        imag_part = partner[:, None, :, 1]
        rotated = jnp.stack([real_part * cos_joint + imag_part * sin_joint, imag_part * cos_joint - real_part * sin_joint], axis=3).astype(jnp.bfloat16)
        left_flat = left_block.reshape(DAYS, BLOCK, -1).astype(jnp.float32)
        rotated_flat = rotated.reshape(DAYS, LAGS, BLOCK, -1).astype(jnp.float32)
        output = jnp.einsum('dck,dlnk->lcn', left_flat, rotated_flat) * norm_factor
        return jnp.where(pair_row[0] >= 0, output, jnp.zeros_like(output))
    result = lax.map(correlate, pair_list)
    return jnp.transpose(result, (1, 0, 2, 3))
```

```python
import functools
import math

import jax
import jax.numpy as jnp
import numpy as np
from jax import lax
from jax.experimental import pallas as pl
from jax.experimental.pallas import tpu as pltpu
from jax.sharding import PartitionSpec as P

BLK_DEV = 2
SEGLEN = 15000
FIRST = 90
HALF_WIN = 64
LSTEP = 25
REACH = 3
BELOW = 1
MESH = pl.DeviceIdType.MESH
VMEM = pl.BlockSpec(memory_space=pltpu.VMEM)
SMEM = pl.BlockSpec(memory_space=pltpu.SMEM)


def phase_tables(lag_total, bin_count):
    lag_samples = (np.arange(lag_total) - lag_total // 2) * LSTEP
    bin_number = FIRST + np.arange(bin_count)
    phase_turns = lag_samples[:, None] * bin_number[None, :] % SEGLEN
    phase_angle = phase_turns.astype(np.float32) * np.float32(2.0 * math.pi / SEGLEN)
    return np.stack([np.cos(phase_angle), np.sin(phase_angle)], axis=1).astype(np.float32)


def mixed(index, offset):
    result = index
    bit = 1
    while bit <= offset:
        if offset & bit:
            result = result + bit - 2 * bit * ((index // bit) % 2)
        bit *= 2
    return result


LANES = 128
ITEM = 32
EARLY = 2


def message_list(channels, item, quarters):
    early = min(EARLY, quarters)
    messages = [(0, early, start, item) for start in range(0, channels, item)]
    for quarter in range(early, quarters):
        size = item if quarter == quarters - 1 else 2 * item
        messages += [(quarter, 1, start, size) for start in range(0, channels, size)]
    return messages


def correlate_kernel(
    tiles, days, group, norm_factor, messages, low_ref, high_ref, own_pair_ref, trig_ref, raw_hbm, out_ref,
    raw_ref, raw_sem, perm_ref, stage_ref, own_ref, spread_ref, win_ref, gath_ref, pair_ref,
    rot_ref, part_ref, day_buf, send_buf, recv_buf, via_buf, top_buf, down_src, down_buf,
    send_sem, recv_sem, far_send, far_recv, pair_send, pair_recv, up_send, up_recv, own_sem,
    day_send, day_recv, tile_send, tile_recv, via_recv, top_send, top_recv, down_send, down_recv,
):
    here = lax.axis_index("tile")
    day = lax.axis_index("day")
    spot = here % group
    base = here - spot
    has_below = base > 0
    has_above = base + group < tiles
    is_top = base + group == tiles
    upper = REACH - BELOW
    last = group - 1
    base_block = (base - BELOW) * BLK_DEV
    window_tiles, quarters, channels, wide = win_ref.shape
    chans = channels // BLK_DEV
    bins = spread_ref.shape[0]
    lags = days
    zero_lag = lags // 2
    rows_dev = out_ref.shape[1]
    item = stage_ref.shape[1] // group
    items = channels // item
    item_rows = raw_ref.shape[0] // items
    perm_rows = perm_ref.shape[0]

    def fetch(index):
        rows = pl.ds(index * item_rows, item_rows)
        return pltpu.make_async_copy(raw_hbm.at[rows], raw_ref.at[rows], raw_sem.at[index])

    for index in range(items):
        fetch(index).start()

    barrier = pltpu.get_barrier_semaphore()
    for offset in range(1, days):
        pl.semaphore_signal(
            barrier, inc=1, device_id={"day": (day + offset) % days}, device_id_type=MESH
        )
    for offset in range(1, group):
        pl.semaphore_signal(
            barrier, inc=1, device_id={"tile": base + mixed(spot, offset)}, device_id_type=MESH
        )

    @pl.when(has_below)
    def _():
        pl.semaphore_signal(barrier, inc=1, device_id={"tile": here - group}, device_id_type=MESH)

    @pl.when(has_above)
    def _():
        pl.semaphore_signal(barrier, inc=1, device_id={"tile": here + group}, device_id_type=MESH)

    row = lax.broadcasted_iota(jnp.int32, (bins, bins), 0)
    col = lax.broadcasted_iota(jnp.int32, (bins, bins), 1)
    spread_ref[...] = jnp.where(jnp.abs(row - col) <= HALF_WIN, 1.0, 0.0).astype(jnp.bfloat16)
    bin_index = lax.broadcasted_iota(jnp.int32, (1, bins), 1)
    counts = (
        jnp.minimum(bin_index + HALF_WIN, bins - 1) - jnp.maximum(bin_index - HALF_WIN, 0) + 1
    ).astype(jnp.float32)
    inverse_counts = 1.0 / counts

    unit = perm_rows // (2 * quarters * group)
    perm_row = lax.broadcasted_iota(jnp.int32, (perm_rows, perm_rows), 0)
    perm_col = lax.broadcasted_iota(jnp.int32, (perm_rows, perm_rows), 1)
    unit_bits = unit.bit_length() - 1
    quarter_bits = quarters.bit_length() - 1
    group_bits = group.bit_length() - 1
    of_unit = perm_row & (unit - 1)
    of_quarter = (perm_row >> unit_bits) & (quarters - 1)
    of_part = (perm_row >> (unit_bits + quarter_bits)) & 1
    of_segment = perm_row >> (unit_bits + quarter_bits + 1)
    source_row = of_segment + (
        (of_quarter + ((of_part + (of_unit << 1)) << quarter_bits)) << group_bits
    )
    perm_ref[...] = jnp.where(source_row == perm_col, 1.0, 0.0).astype(jnp.bfloat16)

    gath_ref[BELOW + spot, 0:2, 0:rows_dev] = own_pair_ref[...]

    @pl.when(base == 0)
    def _():
        gath_ref[0] = jnp.full(gath_ref.shape[1:], -1, jnp.int32)

    peers = days - 1 + group - 1 + has_below.astype(jnp.int32) + has_above.astype(jnp.int32)
    pl.semaphore_wait(barrier, peers)

    def regroup(index):
        sets = item_rows // perm_rows
        for first in range(0, sets, 2):
            start = index * item_rows + first * perm_rows
            pair = jnp.concatenate(
                [
                    raw_ref[start : start + perm_rows],
                    raw_ref[start + perm_rows : start + 2 * perm_rows],
                ],
                axis=1,
            )
            moved = jnp.dot(perm_ref[...], pair, preferred_element_type=jnp.float32)
            for segment in range(group):
                for part in range(2):
                    for quarter in range(quarters):
                        top = ((segment * 2 + part) * quarters + quarter) * unit
                        for half in range(2):
                            target = segment * item + (first + half) * unit
                            stage_ref[
                                part, target : target + unit, quarter * LANES : (quarter + 1) * LANES
                            ] = moved[top : top + unit, half * LANES : (half + 1) * LANES]

    def whiten(index):
        regroup(index)
        real = stage_ref[0]
        imag = stage_ref[1]
        magnitude = jnp.sqrt(real * real + imag * imag)
        coarse = magnitude.astype(jnp.bfloat16)
        fine = (magnitude - coarse.astype(jnp.float32)).astype(jnp.bfloat16)
        both = jnp.dot(
            jnp.concatenate([coarse, fine], axis=0),
            spread_ref[...],
            preferred_element_type=jnp.float32,
        )
        count = group * item
        amplitude = (both[:count] + both[count:]) * inverse_counts + 1e-05
        block = index * item // chans
        keep = (bin_index >= low_ref[block]) & (bin_index < high_ref[block])
        gain = jnp.where(keep, 1.0 / amplitude, 0.0)
        start = index * item
        for part in range(2):
            white = (stage_ref[part] * gain).astype(jnp.bfloat16)
            for segment in range(group):
                for quarter in range(quarters):
                    own_ref[
                        segment, quarter, start : start + item, part * LANES : (part + 1) * LANES
                    ] = white[
                        segment * item : (segment + 1) * item,
                        quarter * LANES : (quarter + 1) * LANES,
                    ]

    def piece(ref, slot, message):
        quarter, count, start, size = messages[message]
        return ref.at[slot, pl.ds(quarter, count), pl.ds(start, size)]

    def across(offset, message):
        there = mixed(spot, offset)
        return pltpu.make_async_remote_copy(
            src_ref=piece(own_ref, there, message),
            dst_ref=piece(win_ref, BELOW + spot, message),
            send_sem=send_sem.at[offset - 1, message],
            recv_sem=recv_sem.at[offset - 1, message],
            device_id={"tile": base + there},
            device_id_type=MESH,
        )

    def pairs_across(offset):
        return pltpu.make_async_remote_copy(
            src_ref=gath_ref.at[BELOW + spot],
            dst_ref=gath_ref.at[BELOW + spot],
            send_sem=pair_send.at[offset - 1],
            recv_sem=pair_recv.at[offset - 1],
            device_id={"tile": base + mixed(spot, offset)},
            device_id_type=MESH,
        )

    def pairs_up():
        return pltpu.make_async_remote_copy(
            src_ref=gath_ref.at[group],
            dst_ref=gath_ref.at[0],
            send_sem=up_send,
            recv_sem=up_recv,
            device_id={"tile": here + group},
            device_id_type=MESH,
        )

    def far(source, slot, target, device, message):
        index = 0 if target == 0 else target - BELOW - group + 1
        return pltpu.make_async_remote_copy(
            src_ref=piece(source, slot, message),
            dst_ref=piece(win_ref, target, message),
            send_sem=far_send.at[index, message],
            recv_sem=far_recv.at[index, message],
            device_id={"tile": device},
            device_id_type=MESH,
        )

    def relay(source, slot, where, message):
        for lower in range(upper):

            @pl.when(has_below & (where == lower))
            def _():
                far(source, slot, BELOW + group + lower, here - group, message).start()

        @pl.when(has_above & (where == last))
        def _():
            far(source, slot, 0, here + group, message).start()

    def send(message):
        for offset in (last, *range(1, last)):
            across(offset, message).start()
        relay(own_ref, spot, spot, message)

    def arrive(message):
        for offset in range(1, group):
            across(offset, message).wait_recv()
            there = mixed(spot, offset)
            relay(win_ref, BELOW + there, there, message)

    def arrive_below(message_range):
        @pl.when(has_below)
        def _():
            for message in message_range:
                far(own_ref, 0, 0, here, message).wait_recv()

    def arrive_above(message_range):
        @pl.when(has_above)
        def _():
            for message in message_range:
                for lower in range(upper):
                    far(own_ref, 0, BELOW + group + lower, here, message).wait_recv()

    def rotate(source, index, slot, quarter):
        span = slice(quarter * LANES, (quarter + 1) * LANES)
        for block in range(BLK_DEV):
            rows = slice(block * chans, (block + 1) * chans)
            target = slot * BLK_DEV + block
            rot_ref[target, zero_lag * chans : (zero_lag + 1) * chans] = source[index, quarter, rows]
            real = source[index, quarter, rows, 0:LANES].astype(jnp.float32)
            imag = source[index, quarter, rows, LANES:wide].astype(jnp.float32)
            for lag in range(lags):
                if lag == zero_lag:
                    continue
                cosine = trig_ref[lag, 0:1, span]
                sine = trig_ref[lag, 1:2, span]
                out_rows = slice(lag * chans, (lag + 1) * chans)
                rot_ref[target, out_rows, 0:LANES] = (real * cosine + imag * sine).astype(jnp.bfloat16)
                rot_ref[target, out_rows, LANES:wide] = (imag * cosine - real * sine).astype(
                    jnp.bfloat16
                )

    def rotate_near(quarter):
        rotate(own_ref, spot, BELOW + spot, quarter)
        for offset in range(1, group):
            slot = BELOW + mixed(spot, offset)
            rotate(win_ref, slot, slot, quarter)

    def rotate_below(quarter):
        for slot in range(BELOW):
            rotate(win_ref, slot, slot, quarter)

    def rotate_above(quarter):
        for slot in range(BELOW + group, window_tiles):
            rotate(win_ref, slot, slot, quarter)

    def product(set_index, row, quarter):
        first = pair_ref[set_index, 0, row]
        second = pair_ref[set_index, 1, row]
        left = jnp.clip(first - base_block, 0, window_tiles * BLK_DEV - 1)
        right = jnp.clip(second - base_block, 0, window_tiles * BLK_DEV - 1)
        total = lax.dot_general(
            rot_ref[left, zero_lag * chans : (zero_lag + 1) * chans],
            rot_ref[right],
            (((1,), (1,)), ((), ())),
            preferred_element_type=jnp.float32,
        )
        for lag in range(lags):
            value = total[:, lag * chans : (lag + 1) * chans]
            if quarter:
                value = value + part_ref[set_index, lag, row]
            if quarter == quarters - 1:
                value = jnp.where(first >= 0, value * norm_factor, 0.0)
            part_ref[set_index, lag, row] = value

    def compute(quarter):
        rotate_near(quarter)
        rotate_below(quarter)
        rotate_above(quarter)

        def one_set(set_index, carry):
            for row in range(rows_dev):
                product(set_index, row, quarter)
            return carry

        lax.fori_loop(0, group + is_top.astype(jnp.int32), one_set, 0)

    for index in range(items):
        fetch(index).wait()
        whiten(index)
        if index:
            send(index - 1)
        else:
            for peer in range(1, group):
                pairs_across(peer).start()
        if index >= 3:
            arrive(index - 3)
    for message in range(items - 1, len(messages)):
        send(message)
    for index in range(max(items - 3, 0), items):
        arrive(index)
    for offset in range(1, group):
        pairs_across(offset).wait()

    @pl.when(has_above)
    def _():
        pairs_up().start()

    by_quarter = [
        [m for m in range(len(messages)) if messages[m][0] <= q < messages[m][0] + messages[m][1]]
        for q in range(quarters)
    ]
    early = messages[0][1]
    pending = [m for m in range(items, len(messages))]
    final = quarters - 1

    def take(count):
        for _ in range(count):
            if pending:
                arrive(pending.pop(0))

    take(len(by_quarter[early]) if early < final else 0)

    @pl.when(has_above)
    def _():
        pairs_up().wait_send()

    @pl.when(has_below)
    def _():
        pairs_up().wait_recv()

    gather_pairs = pltpu.make_async_copy(gath_ref, pair_ref, own_sem)
    gather_pairs.start()
    arrive_below(by_quarter[0])
    arrive_above(by_quarter[0])
    gather_pairs.wait()
    for quarter in range(final):
        if quarter >= early:
            arrive_below(by_quarter[quarter])
            arrive_above(by_quarter[quarter])
        compute(quarter)
        take(len(pending) if quarter == final - 1 else 2 if quarter == final - 2 else len(pending) // 2)
    rotate_near(final)

    def day_copy(step, slot, row):
        target = (day + step) % days
        return pltpu.make_async_remote_copy(
            src_ref=part_ref.at[slot, target, row],
            dst_ref=day_buf.at[step - 1, slot, row],
            send_sem=day_send.at[step - 1, slot, row],
            recv_sem=day_recv.at[step - 1, slot, row],
            device_id={"day": target},
            device_id_type=MESH,
        )

    def day_total(slot, row):
        total = part_ref[slot, day, row]
        for step in range(1, days):
            day_copy(step, slot, row).wait_recv()
            total = total + day_buf[step - 1, slot, row]
        return total

    def to_via(row):
        return pltpu.make_async_remote_copy(
            src_ref=send_buf.at[2, row],
            dst_ref=via_buf.at[row],
            send_sem=tile_send.at[2, row],
            recv_sem=via_recv.at[row],
            device_id={"tile": base + mixed(spot, 1)},
            device_id_type=MESH,
        )

    def to_owner(kind, row):
        return pltpu.make_async_remote_copy(
            src_ref=send_buf.at[kind, row],
            dst_ref=recv_buf.at[kind, row],
            send_sem=tile_send.at[kind, row],
            recv_sem=tile_recv.at[kind, row],
            device_id={"tile": base + mixed(spot, kind + 1)},
            device_id_type=MESH,
        )

    def top_copy(device, slot, row):
        return pltpu.make_async_remote_copy(
            src_ref=send_buf.at[3, row],
            dst_ref=top_buf.at[slot, row],
            send_sem=top_send.at[row],
            recv_sem=top_recv.at[slot, row],
            device_id={"tile": device},
            device_id_type=MESH,
        )

    def down_copy(row, device):
        return pltpu.make_async_remote_copy(
            src_ref=down_src.at[row],
            dst_ref=down_buf.at[row],
            send_sem=down_send.at[row],
            recv_sem=down_recv.at[row],
            device_id={"tile": device},
            device_id_type=MESH,
        )

    outer = (spot == 0) | (spot == last)
    is_outer = outer.astype(jnp.int32)
    sends_down = has_below & (spot == last)
    takes_down = has_above & (spot == last)

    def set_of(target):
        return (target + BELOW) % group

    def choose(one, other):
        return set_of(is_outer * one + (1 - is_outer) * other)

    first_near = choose(mixed(spot, 3), mixed(spot, 1))
    second_near = choose(spot, mixed(spot, 2))
    first_far = choose(mixed(spot, 1), mixed(spot, 3))
    second_far = choose(mixed(spot, 2), spot)

    def finish(slot):
        for row in range(rows_dev):
            product(slot, row, final)
            for step in range(1, days):
                day_copy(step, slot, row).start()

    def push_first(slot, diagonal):
        for row in range(rows_dev):
            total = day_total(slot, row).astype(jnp.bfloat16)

            @pl.when(diagonal)
            def _():
                send_buf[2, row] = total
                to_via(row).start()

            @pl.when(jnp.logical_not(diagonal))
            def _():
                send_buf[0, row] = total
                to_owner(0, row).start()

    def push_via(slot):
        for row in range(rows_dev):
            total = day_total(slot, row)
            to_via(row).wait_recv()
            send_buf[1, row] = (total + via_buf[row].astype(jnp.float32)).astype(jnp.bfloat16)
            to_owner(1, row).start()

    def settle(slot):
        for row in range(rows_dev):
            total = day_total(slot, row)
            for kind in range(2):
                to_owner(kind, row).wait_recv()
                total = total + recv_buf[kind, row].astype(jnp.float32)
            out_ref[0, row] = total

            @pl.when(sends_down)
            def _():
                down_src[row] = total.astype(jnp.bfloat16)
                down_copy(row, here - group).start()

    finish(set_of(0))
    arrive_below(by_quarter[final])
    rotate_below(final)
    finish(set_of(last))
    push_first(first_near, outer)

    @pl.when(is_top)
    def _():
        finish(group)

    arrive_above(by_quarter[final])
    rotate_above(final)
    finish(first_far)

    @pl.when(jnp.logical_not(outer))
    def _():
        push_via(second_near)

    push_first(first_far, jnp.logical_not(outer))

    @pl.when(is_top & (spot < last))
    def _():
        for row in range(rows_dev):
            send_buf[3, row] = day_total(group, row).astype(jnp.bfloat16)
            top_copy(base + last, spot, row).start()

    finish(second_far)

    @pl.when(outer)
    def _():
        settle(second_near)
        push_via(second_far)

    @pl.when(jnp.logical_not(outer))
    def _():
        settle(second_far)

    @pl.when(is_top & (spot == last))
    def _():
        for row in range(rows_dev):
            total = day_total(group, row)
            for slot in range(last):
                top_copy(here, slot, row).wait_recv()
                total = total + top_buf[slot, row].astype(jnp.float32)
            out_ref[0, row] = total

    @pl.when(is_top & (spot < last))
    def _():
        for row in range(rows_dev):
            top_copy(base + last, spot, row).wait_send()

    @pl.when(takes_down)
    def _():
        for row in range(rows_dev):
            down_copy(row, here).wait_recv()
            out_ref[0, row] = down_buf[row].astype(jnp.float32)

    @pl.when(sends_down)
    def _():
        for row in range(rows_dev):
            down_copy(row, here - group).wait_send()

    for row in range(rows_dev):
        to_via(row).wait_send()
        for kind in range(2):
            to_owner(kind, row).wait_send()
        for step in range(1, days):
            for slot in range(group):
                day_copy(step, slot, row).wait_send()

    @pl.when(is_top)
    def _():
        for row in range(rows_dev):
            for step in range(1, days):
                day_copy(step, group, row).wait_send()

    for message in range(len(messages)):
        for offset in range(1, group):
            across(offset, message).wait_send()

    @pl.when(has_above)
    def _():
        for message in range(len(messages)):
            far(own_ref, 0, 0, here + group, message).wait_send()

    @pl.when(has_below)
    def _():
        for message in range(len(messages)):
            for lower in range(upper):
                far(own_ref, 0, BELOW + group + lower, here - group, message).wait_send()


def per_device(tiles, days, spectra, band_low, band_high, pair_list):
    own = spectra[0]
    channels, parts, segments, bins = own.shape
    group = segments
    chans = channels // BLK_DEV
    rows_dev = pair_list.shape[0]
    lags = days
    norm_factor = 1.0 / math.sqrt(segments * bins * days)
    quarters = bins // LANES
    messages = message_list(channels, ITEM, quarters)
    raw = own.reshape(channels, parts, segments, quarters, LANES)
    raw = jnp.transpose(raw, (0, 1, 3, 2, 4)).reshape(-1, LANES)
    perm_rows = 8 * parts * segments * quarters
    count = len(messages)

    block_shape = (rows_dev, chans, chans)
    gathered_shape = (BELOW + group, 8, 128)
    wide = parts * LANES
    return pl.pallas_call(
        functools.partial(correlate_kernel, tiles, days, group, norm_factor, messages),
        out_shape=jax.ShapeDtypeStruct((1,) + block_shape, jnp.float32),
        in_specs=[SMEM, SMEM, VMEM, VMEM, pl.BlockSpec(memory_space=pl.ANY)],
        out_specs=VMEM,
        scratch_shapes=[
            pltpu.VMEM(raw.shape, jnp.bfloat16),
            pltpu.SemaphoreType.DMA((channels // ITEM,)),
            pltpu.VMEM((perm_rows, perm_rows), jnp.bfloat16),
            pltpu.VMEM((parts, segments * ITEM, bins), jnp.float32),
            pltpu.VMEM((segments, quarters, channels, wide), jnp.bfloat16),
            pltpu.VMEM((bins, bins), jnp.bfloat16),
            pltpu.VMEM((group + REACH, quarters, channels, wide), jnp.bfloat16),
            pltpu.VMEM(gathered_shape, jnp.int32),
            pltpu.SMEM(gathered_shape, jnp.int32),
            pltpu.VMEM(((group + REACH) * BLK_DEV, lags * chans, wide), jnp.bfloat16),
            pltpu.VMEM((group + 1, lags) + block_shape, jnp.float32),
            pltpu.VMEM((days - 1, group + 1) + block_shape, jnp.float32),
            pltpu.VMEM((4,) + block_shape, jnp.bfloat16),
            pltpu.VMEM((2,) + block_shape, jnp.bfloat16),
            pltpu.VMEM(block_shape, jnp.bfloat16),
            pltpu.VMEM((group - 1,) + block_shape, jnp.bfloat16),
            pltpu.VMEM(block_shape, jnp.bfloat16),
            pltpu.VMEM(block_shape, jnp.bfloat16),
            pltpu.SemaphoreType.DMA((group - 1, count)),
            pltpu.SemaphoreType.DMA((group - 1, count)),
            pltpu.SemaphoreType.DMA((REACH, count)),
            pltpu.SemaphoreType.DMA((REACH, count)),
            pltpu.SemaphoreType.DMA((group - 1,)),
            pltpu.SemaphoreType.DMA((group - 1,)),
            pltpu.SemaphoreType.DMA,
            pltpu.SemaphoreType.DMA,
            pltpu.SemaphoreType.DMA,
            pltpu.SemaphoreType.DMA((days - 1, group + 1, rows_dev)),
            pltpu.SemaphoreType.DMA((days - 1, group + 1, rows_dev)),
            pltpu.SemaphoreType.DMA((3, rows_dev)),
            pltpu.SemaphoreType.DMA((2, rows_dev)),
            pltpu.SemaphoreType.DMA((rows_dev,)),
            pltpu.SemaphoreType.DMA((rows_dev,)),
            pltpu.SemaphoreType.DMA((group - 1, rows_dev)),
            pltpu.SemaphoreType.DMA((rows_dev,)),
            pltpu.SemaphoreType.DMA((rows_dev,)),
        ],
        compiler_params=pltpu.CompilerParams(
            collective_id=0, has_side_effects=True, vmem_limit_bytes=63 * 1024 * 1024
        ),
    )(band_low, band_high, pair_list.T, jnp.asarray(phase_tables(lags, bins)), raw)


def solution(mesh):
    placed = (P("day", "tile", None, None, None), P("tile"), P("tile"), P("tile", None))
    return jax.shard_map(
        functools.partial(per_device, mesh.shape["tile"], mesh.shape["day"]),
        mesh=mesh,
        in_specs=placed,
        out_specs=P("day", "tile", None, None),
        check_vma=False,
    )
```

```python
import functools
import math

import jax
import jax.numpy as jnp
import numpy as np
from jax import lax
from jax.experimental import pallas as pl
from jax.experimental.pallas import tpu as pltpu
from jax.sharding import PartitionSpec as P

BLK_DEV = 2
SEGLEN = 15000
FIRST = 90
HALF_WIN = 64
LSTEP = 25
REACH = 3
BELOW = 1
MESH = pl.DeviceIdType.MESH
VMEM = pl.BlockSpec(memory_space=pltpu.VMEM)
SMEM = pl.BlockSpec(memory_space=pltpu.SMEM)


def phase_tables(lag_total, bin_count):
    lag_samples = (np.arange(lag_total) - lag_total // 2) * LSTEP
    bin_number = FIRST + np.arange(bin_count)
    phase_turns = lag_samples[:, None] * bin_number[None, :] % SEGLEN
    phase_angle = phase_turns.astype(np.float32) * np.float32(2.0 * math.pi / SEGLEN)
    return np.stack([np.cos(phase_angle), np.sin(phase_angle)], axis=1).astype(np.float32)


def mixed(index, offset):
    result = index
    bit = 1
    while bit <= offset:
        if offset & bit:
            result = result + bit - 2 * bit * ((index // bit) % 2)
        bit *= 2
    return result


LANES = 128
ITEM = 64
EARLY = 2


def message_list(channels, item, quarters):
    early = min(EARLY, quarters)
    messages = [(0, early, start, item) for start in range(0, channels, item)]
    for quarter in range(early, quarters):
        size = item if quarter == quarters - 1 else 2 * item
        messages += [(quarter, 1, start, size) for start in range(0, channels, size)]
    return messages


def correlate_kernel(
    tiles, days, group, norm_factor, messages, low_ref, high_ref, own_pair_ref, trig_ref, raw_hbm, out_ref,
    raw_ref, raw_sem, perm_ref, stage_ref, own_ref, spread_ref, win_ref, gath_ref, pair_ref,
    rot_ref, part_ref, day_buf, send_buf, recv_buf, via_buf, top_buf, down_src, down_buf,
    send_sem, recv_sem, far_send, far_recv, pair_send, pair_recv, up_send, up_recv, own_sem,
    day_send, day_recv, tile_send, tile_recv, via_recv, top_send, top_recv, down_send, down_recv,
):
    here = lax.axis_index("tile")
    day = lax.axis_index("day")
    spot = here % group
    base = here - spot
    has_below = base > 0
    has_above = base + group < tiles
    is_top = base + group == tiles
    upper = REACH - BELOW
    last = group - 1
    base_block = (base - BELOW) * BLK_DEV
    window_tiles, quarters, channels, wide = win_ref.shape
    chans = channels // BLK_DEV
    bins = spread_ref.shape[0]
    lags = days
    zero_lag = lags // 2
    rows_dev = out_ref.shape[1]
    item = stage_ref.shape[1] // group
    items = channels // item
    item_rows = raw_ref.shape[0] // items
    perm_rows = perm_ref.shape[0]

    def fetch(index):
        rows = pl.ds(index * item_rows, item_rows)
        return pltpu.make_async_copy(raw_hbm.at[rows], raw_ref.at[rows], raw_sem.at[index])

    for index in range(items):
        fetch(index).start()

    barrier = pltpu.get_barrier_semaphore()
    for offset in range(1, days):
        pl.semaphore_signal(
            barrier, inc=1, device_id={"day": (day + offset) % days}, device_id_type=MESH
        )
    for offset in range(1, group):
        pl.semaphore_signal(
            barrier, inc=1, device_id={"tile": base + mixed(spot, offset)}, device_id_type=MESH
        )

    @pl.when(has_below)
    def _():
        pl.semaphore_signal(barrier, inc=1, device_id={"tile": here - group}, device_id_type=MESH)

    @pl.when(has_above)
    def _():
        pl.semaphore_signal(barrier, inc=1, device_id={"tile": here + group}, device_id_type=MESH)

    row = lax.broadcasted_iota(jnp.int32, (bins, bins), 0)
    col = lax.broadcasted_iota(jnp.int32, (bins, bins), 1)
    spread_ref[...] = jnp.where(jnp.abs(row - col) <= HALF_WIN, 1.0, 0.0).astype(jnp.bfloat16)
    bin_index = lax.broadcasted_iota(jnp.int32, (1, bins), 1)
    counts = (
        jnp.minimum(bin_index + HALF_WIN, bins - 1) - jnp.maximum(bin_index - HALF_WIN, 0) + 1
    ).astype(jnp.float32)
    inverse_counts = 1.0 / counts

    unit = perm_rows // (2 * quarters * group)
    perm_row = lax.broadcasted_iota(jnp.int32, (perm_rows, perm_rows), 0)
    perm_col = lax.broadcasted_iota(jnp.int32, (perm_rows, perm_rows), 1)
    unit_bits = unit.bit_length() - 1
    quarter_bits = quarters.bit_length() - 1
    group_bits = group.bit_length() - 1
    of_unit = perm_row & (unit - 1)
    of_quarter = (perm_row >> unit_bits) & (quarters - 1)
    of_part = (perm_row >> (unit_bits + quarter_bits)) & 1
    of_segment = perm_row >> (unit_bits + quarter_bits + 1)
    source_row = of_segment + (
        (of_quarter + ((of_part + (of_unit << 1)) << quarter_bits)) << group_bits
    )
    perm_ref[...] = jnp.where(source_row == perm_col, 1.0, 0.0).astype(jnp.bfloat16)

    gath_ref[BELOW + spot, 0:2, 0:rows_dev] = own_pair_ref[...]

    @pl.when(base == 0)
    def _():
        gath_ref[0] = jnp.full(gath_ref.shape[1:], -1, jnp.int32)

    peers = days - 1 + group - 1 + has_below.astype(jnp.int32) + has_above.astype(jnp.int32)
    pl.semaphore_wait(barrier, peers)

    def regroup(index):
        sets = item_rows // perm_rows
        for first in range(0, sets, 2):
            start = index * item_rows + first * perm_rows
            pair = jnp.concatenate(
                [
                    raw_ref[start : start + perm_rows],
                    raw_ref[start + perm_rows : start + 2 * perm_rows],
                ],
                axis=1,
            )
            moved = jnp.dot(perm_ref[...], pair, preferred_element_type=jnp.float32)
            for segment in range(group):
                for part in range(2):
                    for quarter in range(quarters):
                        top = ((segment * 2 + part) * quarters + quarter) * unit
                        for half in range(2):
                            target = segment * item + (first + half) * unit
                            stage_ref[
                                part, target : target + unit, quarter * LANES : (quarter + 1) * LANES
                            ] = moved[top : top + unit, half * LANES : (half + 1) * LANES]

    def whiten(index):
        regroup(index)
        real = stage_ref[0]
        imag = stage_ref[1]
        magnitude = jnp.sqrt(real * real + imag * imag)
        coarse = magnitude.astype(jnp.bfloat16)
        fine = (magnitude - coarse.astype(jnp.float32)).astype(jnp.bfloat16)
        both = jnp.dot(
            jnp.concatenate([coarse, fine], axis=0),
            spread_ref[...],
            preferred_element_type=jnp.float32,
        )
        count = group * item
        amplitude = (both[:count] + both[count:]) * inverse_counts + 1e-05
        block = index * item // chans
        keep = (bin_index >= low_ref[block]) & (bin_index < high_ref[block])
        gain = jnp.where(keep, 1.0 / amplitude, 0.0)
        start = index * item
        for part in range(2):
            white = (stage_ref[part] * gain).astype(jnp.bfloat16)
            for segment in range(group):
                for quarter in range(quarters):
                    own_ref[
                        segment, quarter, start : start + item, part * LANES : (part + 1) * LANES
                    ] = white[
                        segment * item : (segment + 1) * item,
                        quarter * LANES : (quarter + 1) * LANES,
                    ]

    def piece(ref, slot, message):
        quarter, count, start, size = messages[message]
        return ref.at[slot, pl.ds(quarter, count), pl.ds(start, size)]

    def across(offset, message):
        there = mixed(spot, offset)
        return pltpu.make_async_remote_copy(
            src_ref=piece(own_ref, there, message),
            dst_ref=piece(win_ref, BELOW + spot, message),
            send_sem=send_sem.at[offset - 1, message],
            recv_sem=recv_sem.at[offset - 1, message],
            device_id={"tile": base + there},
            device_id_type=MESH,
        )

    def pairs_across(offset):
        return pltpu.make_async_remote_copy(
            src_ref=gath_ref.at[BELOW + spot],
            dst_ref=gath_ref.at[BELOW + spot],
            send_sem=pair_send.at[offset - 1],
            recv_sem=pair_recv.at[offset - 1],
            device_id={"tile": base + mixed(spot, offset)},
            device_id_type=MESH,
        )

    def pairs_up():
        return pltpu.make_async_remote_copy(
            src_ref=gath_ref.at[group],
            dst_ref=gath_ref.at[0],
            send_sem=up_send,
            recv_sem=up_recv,
            device_id={"tile": here + group},
            device_id_type=MESH,
        )

    def far(source, slot, target, device, message):
        index = 0 if target == 0 else target - BELOW - group + 1
        return pltpu.make_async_remote_copy(
            src_ref=piece(source, slot, message),
            dst_ref=piece(win_ref, target, message),
            send_sem=far_send.at[index, message],
            recv_sem=far_recv.at[index, message],
            device_id={"tile": device},
            device_id_type=MESH,
        )

    def relay(source, slot, where, message):
        for lower in range(upper):

            @pl.when(has_below & (where == lower))
            def _():
                far(source, slot, BELOW + group + lower, here - group, message).start()

        @pl.when(has_above & (where == last))
        def _():
            far(source, slot, 0, here + group, message).start()

    def send(message):
        for offset in (last, *range(1, last)):
            across(offset, message).start()
        relay(own_ref, spot, spot, message)

    def arrive(message):
        for offset in range(1, group):
            across(offset, message).wait_recv()
            there = mixed(spot, offset)
            relay(win_ref, BELOW + there, there, message)

    def arrive_below(message_range):
        @pl.when(has_below)
        def _():
            for message in message_range:
                far(own_ref, 0, 0, here, message).wait_recv()

    def arrive_above(message_range):
        @pl.when(has_above)
        def _():
            for message in message_range:
                for lower in range(upper):
                    far(own_ref, 0, BELOW + group + lower, here, message).wait_recv()

    def rotate(source, index, slot, quarter):
        span = slice(quarter * LANES, (quarter + 1) * LANES)
        for block in range(BLK_DEV):
            rows = slice(block * chans, (block + 1) * chans)
            target = slot * BLK_DEV + block
            rot_ref[target, zero_lag * chans : (zero_lag + 1) * chans] = source[index, quarter, rows]
            real = source[index, quarter, rows, 0:LANES].astype(jnp.float32)
            imag = source[index, quarter, rows, LANES:wide].astype(jnp.float32)
            for lag in range(lags):
                if lag == zero_lag:
                    continue
                cosine = trig_ref[lag, 0:1, span]
                sine = trig_ref[lag, 1:2, span]
                out_rows = slice(lag * chans, (lag + 1) * chans)
                rot_ref[target, out_rows, 0:LANES] = (real * cosine + imag * sine).astype(jnp.bfloat16)
                rot_ref[target, out_rows, LANES:wide] = (imag * cosine - real * sine).astype(
                    jnp.bfloat16
                )

    def rotate_near(quarter):
        rotate(own_ref, spot, BELOW + spot, quarter)
        for offset in range(1, group):
            slot = BELOW + mixed(spot, offset)
            rotate(win_ref, slot, slot, quarter)

    def rotate_below(quarter):
        for slot in range(BELOW):
            rotate(win_ref, slot, slot, quarter)

    def rotate_above(quarter):
        for slot in range(BELOW + group, window_tiles):
            rotate(win_ref, slot, slot, quarter)

    def product(set_index, row, quarter):
        first = pair_ref[set_index, 0, row]
        second = pair_ref[set_index, 1, row]
        left = jnp.clip(first - base_block, 0, window_tiles * BLK_DEV - 1)
        right = jnp.clip(second - base_block, 0, window_tiles * BLK_DEV - 1)
        total = lax.dot_general(
            rot_ref[left, zero_lag * chans : (zero_lag + 1) * chans],
            rot_ref[right],
            (((1,), (1,)), ((), ())),
            preferred_element_type=jnp.float32,
        )
        for lag in range(lags):
            value = total[:, lag * chans : (lag + 1) * chans]
            if quarter:
                value = value + part_ref[set_index, lag, row]
            if quarter == quarters - 1:
                value = jnp.where(first >= 0, value * norm_factor, 0.0)
            part_ref[set_index, lag, row] = value

    def compute(quarter):
        rotate_near(quarter)
        rotate_below(quarter)
        rotate_above(quarter)

        def one_set(set_index, carry):
            for row in range(rows_dev):
                product(set_index, row, quarter)
            return carry

        lax.fori_loop(0, group + is_top.astype(jnp.int32), one_set, 0)

    for index in range(items):
        fetch(index).wait()
        whiten(index)
        if index:
            send(index - 1)
        else:
            for peer in range(1, group):
                pairs_across(peer).start()
        if index >= 3:
            arrive(index - 3)
    for message in range(items - 1, len(messages)):
        send(message)
    for index in range(max(items - 3, 0), items):
        arrive(index)
    for offset in range(1, group):
        pairs_across(offset).wait()

    @pl.when(has_above)
    def _():
        pairs_up().start()

    by_quarter = [
        [m for m in range(len(messages)) if messages[m][0] <= q < messages[m][0] + messages[m][1]]
        for q in range(quarters)
    ]
    early = messages[0][1]
    pending = [m for m in range(items, len(messages))]
    final = quarters - 1

    def take(count):
        for _ in range(count):
            if pending:
                arrive(pending.pop(0))

    take(len(by_quarter[early]) if early < final else 0)

    @pl.when(has_above)
    def _():
        pairs_up().wait_send()

    @pl.when(has_below)
    def _():
        pairs_up().wait_recv()

    gather_pairs = pltpu.make_async_copy(gath_ref, pair_ref, own_sem)
    gather_pairs.start()
    arrive_below(by_quarter[0])
    arrive_above(by_quarter[0])
    gather_pairs.wait()
    for quarter in range(final):
        if quarter >= early:
            arrive_below(by_quarter[quarter])
            arrive_above(by_quarter[quarter])
        compute(quarter)
        take(len(pending) if quarter == final - 1 else 2 if quarter == final - 2 else len(pending) // 2)
    rotate_near(final)

    def day_copy(step, slot, row):
        target = (day + step) % days
        return pltpu.make_async_remote_copy(
            src_ref=part_ref.at[slot, target, row],
            dst_ref=day_buf.at[step - 1, slot, row],
            send_sem=day_send.at[step - 1, slot, row],
            recv_sem=day_recv.at[step - 1, slot, row],
            device_id={"day": target},
            device_id_type=MESH,
        )

    def day_total(slot, row):
        total = part_ref[slot, day, row]
        for step in range(1, days):
            day_copy(step, slot, row).wait_recv()
            total = total + day_buf[step - 1, slot, row]
        return total

    def to_via(row):
        return pltpu.make_async_remote_copy(
            src_ref=send_buf.at[2, row],
            dst_ref=via_buf.at[row],
            send_sem=tile_send.at[2, row],
            recv_sem=via_recv.at[row],
            device_id={"tile": base + mixed(spot, 1)},
            device_id_type=MESH,
        )

    def to_owner(kind, row):
        return pltpu.make_async_remote_copy(
            src_ref=send_buf.at[kind, row],
            dst_ref=recv_buf.at[kind, row],
            send_sem=tile_send.at[kind, row],
            recv_sem=tile_recv.at[kind, row],
            device_id={"tile": base + mixed(spot, kind + 1)},
            device_id_type=MESH,
        )

    def top_copy(device, slot, row):
        return pltpu.make_async_remote_copy(
            src_ref=send_buf.at[3, row],
            dst_ref=top_buf.at[slot, row],
            send_sem=top_send.at[row],
            recv_sem=top_recv.at[slot, row],
            device_id={"tile": device},
            device_id_type=MESH,
        )

    def down_copy(row, device):
        return pltpu.make_async_remote_copy(
            src_ref=down_src.at[row],
            dst_ref=down_buf.at[row],
            send_sem=down_send.at[row],
            recv_sem=down_recv.at[row],
            device_id={"tile": device},
            device_id_type=MESH,
        )

    outer = (spot == 0) | (spot == last)
    is_outer = outer.astype(jnp.int32)
    sends_down = has_below & (spot == last)
    takes_down = has_above & (spot == last)

    def set_of(target):
        return (target + BELOW) % group

    def choose(one, other):
        return set_of(is_outer * one + (1 - is_outer) * other)

    first_near = choose(mixed(spot, 3), mixed(spot, 1))
    second_near = choose(spot, mixed(spot, 2))
    first_far = choose(mixed(spot, 1), mixed(spot, 3))
    second_far = choose(mixed(spot, 2), spot)

    def finish(slot):
        for row in range(rows_dev):
            product(slot, row, final)
            for step in range(1, days):
                day_copy(step, slot, row).start()

    def push_first(slot, diagonal):
        for row in range(rows_dev):
            total = day_total(slot, row).astype(jnp.bfloat16)

            @pl.when(diagonal)
            def _():
                send_buf[2, row] = total
                to_via(row).start()

            @pl.when(jnp.logical_not(diagonal))
            def _():
                send_buf[0, row] = total
                to_owner(0, row).start()

    def push_via(slot, chosen):
        for row in chosen:
            total = day_total(slot, row)
            to_via(row).wait_recv()
            send_buf[1, row] = (total + via_buf[row].astype(jnp.float32)).astype(jnp.bfloat16)
            to_owner(1, row).start()

    def settle(slot, chosen):
        for row in chosen:
            total = day_total(slot, row)
            for kind in range(2):
                to_owner(kind, row).wait_recv()
                total = total + recv_buf[kind, row].astype(jnp.float32)
            out_ref[0, row] = total

            @pl.when(sends_down)
            def _():
                down_src[row] = total.astype(jnp.bfloat16)
                down_copy(row, here - group).start()

    finish(set_of(0))
    arrive_below(by_quarter[final])
    rotate_below(final)
    finish(set_of(last))
    push_first(first_near, outer)

    @pl.when(is_top)
    def _():
        finish(group)

    arrive_above(by_quarter[final])
    rotate_above(final)
    finish(first_far)

    push_first(first_far, jnp.logical_not(outer))

    @pl.when(jnp.logical_not(outer))
    def _():
        push_via(second_near, range(rows_dev))

    finish(second_far)

    @pl.when(is_top & (spot < last))
    def _():
        for row in range(rows_dev):
            send_buf[3, row] = day_total(group, row).astype(jnp.bfloat16)
            top_copy(base + last, spot, row).start()

    @pl.when(outer)
    def _():
        for row in range(rows_dev):
            settle(second_near, [row])
            push_via(second_far, [row])

    @pl.when(jnp.logical_not(outer))
    def _():
        settle(second_far, range(rows_dev))

    @pl.when(is_top & (spot == last))
    def _():
        for row in range(rows_dev):
            total = day_total(group, row)
            for slot in range(last):
                top_copy(here, slot, row).wait_recv()
                total = total + top_buf[slot, row].astype(jnp.float32)
            out_ref[0, row] = total

    @pl.when(is_top & (spot < last))
    def _():
        for row in range(rows_dev):
            top_copy(base + last, spot, row).wait_send()

    @pl.when(takes_down)
    def _():
        for row in range(rows_dev):
            down_copy(row, here).wait_recv()
            out_ref[0, row] = down_buf[row].astype(jnp.float32)

    @pl.when(sends_down)
    def _():
        for row in range(rows_dev):
            down_copy(row, here - group).wait_send()

    for row in range(rows_dev):
        to_via(row).wait_send()
        for kind in range(2):
            to_owner(kind, row).wait_send()
        for step in range(1, days):
            for slot in range(group):
                day_copy(step, slot, row).wait_send()

    @pl.when(is_top)
    def _():
        for row in range(rows_dev):
            for step in range(1, days):
                day_copy(step, group, row).wait_send()

    for message in range(len(messages)):
        for offset in range(1, group):
            across(offset, message).wait_send()

    @pl.when(has_above)
    def _():
        for message in range(len(messages)):
            far(own_ref, 0, 0, here + group, message).wait_send()

    @pl.when(has_below)
    def _():
        for message in range(len(messages)):
            for lower in range(upper):
                far(own_ref, 0, BELOW + group + lower, here - group, message).wait_send()


def per_device(tiles, days, spectra, band_low, band_high, pair_list):
    own = spectra[0]
    channels, parts, segments, bins = own.shape
    group = segments
    chans = channels // BLK_DEV
    rows_dev = pair_list.shape[0]
    lags = days
    norm_factor = 1.0 / math.sqrt(segments * bins * days)
    quarters = bins // LANES
    messages = message_list(channels, ITEM, quarters)
    raw = own.reshape(channels, parts, segments, quarters, LANES)
    raw = jnp.transpose(raw, (0, 1, 3, 2, 4)).reshape(-1, LANES)
    perm_rows = 8 * parts * segments * quarters
    count = len(messages)

    block_shape = (rows_dev, chans, chans)
    gathered_shape = (BELOW + group, 8, 128)
    wide = parts * LANES
    return pl.pallas_call(
        functools.partial(correlate_kernel, tiles, days, group, norm_factor, messages),
        out_shape=jax.ShapeDtypeStruct((1,) + block_shape, jnp.float32),
        in_specs=[SMEM, SMEM, VMEM, VMEM, pl.BlockSpec(memory_space=pl.ANY)],
        out_specs=VMEM,
        scratch_shapes=[
            pltpu.VMEM(raw.shape, jnp.bfloat16),
            pltpu.SemaphoreType.DMA((channels // ITEM,)),
            pltpu.VMEM((perm_rows, perm_rows), jnp.bfloat16),
            pltpu.VMEM((parts, segments * ITEM, bins), jnp.float32),
            pltpu.VMEM((segments, quarters, channels, wide), jnp.bfloat16),
            pltpu.VMEM((bins, bins), jnp.bfloat16),
            pltpu.VMEM((group + REACH, quarters, channels, wide), jnp.bfloat16),
            pltpu.VMEM(gathered_shape, jnp.int32),
            pltpu.SMEM(gathered_shape, jnp.int32),
            pltpu.VMEM(((group + REACH) * BLK_DEV, lags * chans, wide), jnp.bfloat16),
            pltpu.VMEM((group + 1, lags) + block_shape, jnp.float32),
            pltpu.VMEM((days - 1, group + 1) + block_shape, jnp.float32),
            pltpu.VMEM((4,) + block_shape, jnp.bfloat16),
            pltpu.VMEM((2,) + block_shape, jnp.bfloat16),
            pltpu.VMEM(block_shape, jnp.bfloat16),
            pltpu.VMEM((group - 1,) + block_shape, jnp.bfloat16),
            pltpu.VMEM(block_shape, jnp.bfloat16),
            pltpu.VMEM(block_shape, jnp.bfloat16),
            pltpu.SemaphoreType.DMA((group - 1, count)),
            pltpu.SemaphoreType.DMA((group - 1, count)),
            pltpu.SemaphoreType.DMA((REACH, count)),
            pltpu.SemaphoreType.DMA((REACH, count)),
            pltpu.SemaphoreType.DMA((group - 1,)),
            pltpu.SemaphoreType.DMA((group - 1,)),
            pltpu.SemaphoreType.DMA,
            pltpu.SemaphoreType.DMA,
            pltpu.SemaphoreType.DMA,
            pltpu.SemaphoreType.DMA((days - 1, group + 1, rows_dev)),
            pltpu.SemaphoreType.DMA((days - 1, group + 1, rows_dev)),
            pltpu.SemaphoreType.DMA((3, rows_dev)),
            pltpu.SemaphoreType.DMA((2, rows_dev)),
            pltpu.SemaphoreType.DMA((rows_dev,)),
            pltpu.SemaphoreType.DMA((rows_dev,)),
            pltpu.SemaphoreType.DMA((group - 1, rows_dev)),
            pltpu.SemaphoreType.DMA((rows_dev,)),
            pltpu.SemaphoreType.DMA((rows_dev,)),
        ],
        compiler_params=pltpu.CompilerParams(
            collective_id=0, has_side_effects=True, vmem_limit_bytes=63 * 1024 * 1024
        ),
    )(band_low, band_high, pair_list.T, jnp.asarray(phase_tables(lags, bins)), raw)


def solution(mesh):
    placed = (P("day", "tile", None, None, None), P("tile"), P("tile"), P("tile", None))
    return jax.shard_map(
        functools.partial(per_device, mesh.shape["tile"], mesh.shape["day"]),
        mesh=mesh,
        in_specs=placed,
        out_specs=P("day", "tile", None, None),
        check_vma=False,
    )
```
